32 devices in a mesh: rows: 8 (over z, x), rhs: 4 (over y, core).
Axes of the slice: x: 2, y: 2, z: 4, core: 2. Of those that a mesh axis runs over, the one named last changes fastest.
Arguments:
- right_side: float32 [4, 64, 256, 256], P(None, 'rows', 'rhs'), parts along dimension 2, may hold values from -6 to 6
- prior: float32 [64, 256, 256], P('rows', 'rhs'), parts along dimension 1, may hold values from -6 to 6
- lower_blocks: float32 [4, 64, 4, 256, 256], P(None, 'rows'), may hold values from -0.09375 to 0.09375
- inverse_diag: float32 [4, 64, 256, 256], P(None, 'rows'), may hold values from -0.375 to 0.375
- fill_cols: int32 [4, 64, 4], P(None, 'rows'), may hold values from -1 to 255, as said below
Outputs:
- solution: float32 [4, 64, 256, 256], P(None, 'rows', 'rhs'), parts along dimension 2
The draws below stay inside these ranges and needn't reach their ends.
There are 4 independent parts, one for each index of `rhs`. The reference program is written for one: setup_inputs(seed, part) draws one part's arguments, and reference() takes and returns one part's arrays. A program takes and returns all parts, laid end to end along the dimension named above; an argument that names none is the same for every part. Nothing has to cross between parts.
Inputs may be any that keep to these rules, and one draw needn't show every extreme that they name: `fill_cols`: for block row j of level l, held at index d = j // 8 of rows with position k = j % 8: every filled slot names a panel of the level before (the prior panels for l = 0), numbered l * 64 + e * 8 + k2, whose holder e is d, d XOR 2^a or d XOR 2^b, where a = 2l mod log2 of the rows axis size and b = (2l + 1) mod log2 of it. Slot 0 names position k at holder d XOR 2^a, slot 1 position k at holder d XOR 2^b; the further slots name distinct other panels of these three holders, and filled slots come first, followed by -1.
All inputs are finite; a program needn't handle non-finite values.
Results may differ from the reference program's by a relative error of at most 0.0001.
Values sent between devices are 32-bit elements; how exact they have to be, the bound alone decides.
A program may use at most 192 MiB of HBM per device.

```python
import jax
import jax.numpy as jnp
from jax import lax

BS = 256
NRHS = 64
LEV = 4
FILL = 4
LB_DEV = 8
NL = 64


def draw_fill_cols(key, part):
    per_dev = LB_DEV
    devices = NL // LB_DEV
    bit_count = devices.bit_length() - 1
    heights = jnp.arange(LEV, dtype=jnp.int32)[:, None]
    positions = jnp.arange(NL, dtype=jnp.int32)[None, :]
    holder = positions // per_dev
    within = positions % per_dev
    first_bit = 2 * heights % bit_count
    second_bit = (2 * heights + 1) % bit_count
    first_partner = jnp.bitwise_xor(holder, jnp.left_shift(jnp.int32(1), first_bit))
    second_partner = jnp.bitwise_xor(holder, jnp.left_shift(jnp.int32(1), second_bit))
    level_base = heights * NL
    slot_first = level_base + first_partner * per_dev + within
    slot_second = level_base + second_partner * per_dev + within
    choice_total = 3 * per_dev
    candidate = jnp.arange(choice_total, dtype=jnp.int32)[None, None, :]
    cand_holder = jnp.where(candidate < per_dev, holder[:, :, None], jnp.where(candidate < 2 * per_dev, first_partner[:, :, None], second_partner[:, :, None]))
    cand_within = candidate % per_dev
    cand_global = level_base[:, :, None] + cand_holder * per_dev + cand_within
    excluded = (candidate >= per_dev) & (cand_within == within[:, :, None])
    score_key, count_key = jax.random.split(key)
    scores = jax.random.randint(score_key, (LEV, NL, choice_total), 0, 1 << 20, dtype=jnp.int32) * choice_total + candidate
    scores = jnp.where(excluded, -1 - candidate, scores)
    best_scores, chosen = lax.top_k(scores, FILL - 2)
    further = jnp.take_along_axis(cand_global, chosen, axis=2)
    counts = jax.random.randint(count_key, (LEV, NL), 2, FILL + 1, dtype=jnp.int32)
    counts = counts.at[:, 0].set(2).at[:, 1].set(FILL)
    slot_ids = jnp.arange(FILL, dtype=jnp.int32)[None, None, :]
    proposal = jnp.concatenate([slot_first[:, :, None], slot_second[:, :, None], further], axis=2)
    return jnp.where(slot_ids < counts[:, :, None], proposal, -1).astype(jnp.int32)


def steps_of(key, shape, pieces, smallest, top_value):
    level, own = 1.0, jax.random.fold_in(key, 6)
    for axis_at, parts in pieces:
        steps = jnp.exp(jax.random.uniform(jax.random.fold_in(own, axis_at), (parts,), jnp.float32, smallest / len(pieces), top_value / len(pieces)))
        level = level * jnp.repeat(steps, shape[axis_at] // parts).reshape([-1 if axis == axis_at else 1 for axis in range(len(shape))])
    return level


def noise(stream_key, extent, scale, most, pieces=(), held_as=jnp.bfloat16):
    drawn = scale * jax.random.normal(stream_key, extent, jnp.float32)
    if pieces:
        drawn = drawn * steps_of(stream_key, extent, pieces, -0.22, 0.18)
    return jnp.clip(drawn, -most, most).astype(held_as)


def setup_inputs(seed: int = 0, part: int = 0) -> dict:
    splits = jax.random.split(jax.random.key(seed), 6)
    part_keys = jax.random.split(jax.random.fold_in(splits[5], part), 6)
    return {
        "right_side": noise(part_keys[0], (LEV, NL, NRHS, BS), 1.0, 6.0, ((1, 8),), jnp.float32),
        "prior": noise(part_keys[1], (NL, NRHS, BS), 1.0, 6.0, ((0, 8),), jnp.float32),
        "lower_blocks": noise(splits[2], (LEV, NL, FILL, BS, BS), (4 * BS * FILL) ** -0.5, 0.09375, ((1, 8),), jnp.float32),
        "inverse_diag": noise(splits[3], (LEV, NL, BS, BS), BS ** -0.5, 0.375, ((1, 8),), jnp.float32),
        "fill_cols": draw_fill_cols(jax.random.fold_in(splits[5], 71), part),
    }


def reference(right_side, prior, lower_blocks, inverse_diag, fill_cols):
    highest = lax.Precision.HIGHEST
    segment_table = prior
    solved = []
    for height in range(LEV):
        columns = fill_cols[height]
        filled = columns >= 0
        position = jnp.where(filled, columns - height * NL, 0).astype(jnp.int32)
        picked = segment_table[position] * filled[:, :, None, None].astype(jnp.float32)
        contribution = jnp.einsum("jfnc,jfrc->jnr", picked, lower_blocks[height], precision=highest)
        reduced = right_side[height] - contribution
        current = jnp.einsum("jnc,jrc->jnr", reduced, inverse_diag[height], precision=highest)
        solved.append(current)
        segment_table = current
    return jnp.stack(solved)
```

```python
import functools

import jax
import jax.numpy as jnp
from jax import lax
from jax.experimental import pallas as pl
from jax.experimental.pallas import tpu as pltpu
from jax.sharding import PartitionSpec as P

CHUNKS = 2
STAGE = 6
KEPT = 3


def split(x):
    high = x.astype(jnp.bfloat16)
    low = (x - high.astype(jnp.float32)).astype(jnp.bfloat16)
    return high, low


def times_transposed(left, right):
    return lax.dot_general(
        left, right, (((1,), (1,)), ((), ())), preferred_element_type=jnp.float32
    )


def product(panel, high, low):
    count = panel.shape[0]
    panel_high, panel_low = split(panel)
    both = times_transposed(jnp.concatenate([panel_high, panel_low], axis=0), high)
    return both[:count] + both[count:] + times_transposed(panel_high, low)


def kernel(
    right_hbm, prior_hbm, lower_hbm, inverse_hbm, fill, out_hbm,
    tables, last, right, stage, high_blocks, low_blocks,
    stage_sem, right_sem, prior_sem, send_sem, recv_sem, out_sem,
):
    levels, per_dev, fills = fill.shape
    devices = lax.axis_size("rows")
    bits = devices.bit_length() - 1
    me = lax.axis_index("rows")
    width = right.shape[2] // CHUNKS
    units = levels * per_dev
    partners = [
        [jnp.bitwise_xor(me, 1 << (2 * l + j) % bits) for j in range(2)] for l in range(levels)
    ]

    def stage_copies(unit):
        level, row, slot = unit // per_dev, unit % per_dev, unit % STAGE
        return (
            pltpu.make_async_copy(
                lower_hbm.at[level, row], stage.at[slot, pl.ds(0, fills)], stage_sem.at[0, slot]
            ),
            pltpu.make_async_copy(
                inverse_hbm.at[level, row], stage.at[slot, fills], stage_sem.at[1, slot]
            ),
        )

    def rows_of(c):
        return pl.ds(c * width, width)

    def prior_send(c, j):
        return pltpu.make_async_remote_copy(
            src_ref=prior_hbm.at[:, rows_of(c)],
            dst_ref=tables[0][c].at[pl.ds((j + 1) * per_dev, per_dev)],
            send_sem=send_sem.at[0, c, j],
            recv_sem=recv_sem.at[0, c, j],
            device_id={"rows": partners[0][j]},
            device_id_type=pl.DeviceIdType.MESH,
        )

    def panel_send(l, c, j, first, count):
        table = tables[l][c]
        return pltpu.make_async_remote_copy(
            src_ref=table.at[pl.ds(first, count)],
            dst_ref=table.at[pl.ds((j + 1) * per_dev + first, count)],
            send_sem=send_sem.at[l, c, j],
            recv_sem=recv_sem.at[l, c, j],
            device_id={"rows": partners[l][j]},
            device_id_type=pl.DeviceIdType.MESH,
        )

    def solved(l, c):
        return last[c] if l == levels - 1 else tables[l + 1][c].at[pl.ds(0, per_dev)]

    def out_copy(l, c):
        return pltpu.make_async_copy(
            solved(l, c), out_hbm.at[l, :, rows_of(c)], out_sem.at[l, c]
        )

    def prior_copy(c):
        return pltpu.make_async_copy(
            prior_hbm.at[:, rows_of(c)], tables[0][c].at[pl.ds(0, per_dev)], prior_sem.at[c]
        )

    def right_copy(l):
        return pltpu.make_async_copy(right_hbm.at[l], right.at[l], right_sem.at[l])

    def convert(level):
        kept = level % KEPT

        def one(row, carry):
            unit = level * per_dev + row
            slot = unit % STAGE
            for copy in stage_copies(unit):
                copy.wait()

            def block(b, inner):
                high, low = split(stage[slot, b])
                high_blocks[kept, row, b] = high
                low_blocks[kept, row, b] = low
                return inner

            lax.fori_loop(0, fills + 1, block, 0)

            @pl.when(unit + STAGE < units)
            def _():
                for copy in stage_copies(unit + STAGE):
                    copy.start()

            return carry

        lax.fori_loop(0, per_dev, one, 0)

    def step(l, c):
        kept = l % KEPT
        if l == 0:
            prior_copy(c).wait()
        if c == 0:
            right_copy(l).wait()
        for j in range(2):
            panel_send(l, c, j, 0, per_dev).wait_recv()
        table = tables[l][c]

        def one(row, carry):
            total = jnp.zeros((width, right.shape[3]), jnp.float32)
            for f in range(fills):
                column = fill[l, row, f]
                relative = jnp.maximum(column - l * devices * per_dev, 0)
                holder, within = relative // per_dev, relative % per_dev
                group = jnp.where(
                    holder == me, 0, jnp.where(holder == partners[l][0], 1, 2)
                )
                filled = jnp.where(column >= 0, 1.0, 0.0).astype(jnp.float32)
                panel = table[group * per_dev + within] * filled
                total += product(panel, high_blocks[kept, row, f], low_blocks[kept, row, f])
            reduced = right[l, row, rows_of(c)] - total
            current = product(
                reduced, high_blocks[kept, row, fills], low_blocks[kept, row, fills]
            )
            if l == levels - 1:
                last[c][row] = current
            else:
                tables[l + 1][c][row] = current
                for j in range(2):
                    panel_send(l + 1, c, j, row, 1).start()
            return carry

        lax.fori_loop(0, per_dev, one, 0)
        out_copy(l, c).start()

    for unit in range(min(STAGE, units)):
        for copy in stage_copies(unit):
            copy.start()
    for c in range(CHUNKS):
        prior_copy(c).start()
    for l in range(levels):
        right_copy(l).start()

    barrier = pltpu.get_barrier_semaphore()
    for bit in range(bits):
        pl.semaphore_signal(
            barrier,
            inc=1,
            device_id={"rows": jnp.bitwise_xor(me, 1 << bit)},
            device_id_type=pl.DeviceIdType.MESH,
        )
    pl.semaphore_wait(barrier, bits)

    for c in range(CHUNKS):
        for j in range(2):
            prior_send(c, j).start()
    for level in range(min(2, levels)):
        convert(level)
    for l in range(levels):
        for c in range(CHUNKS):
            step(l, c)
            if l == 0 and c == 0 and levels > 2:
                convert(2)
        if l + 3 < levels:
            convert(l + 3)
    for c in range(CHUNKS):
        for j in range(2):
            prior_send(c, j).wait_send()
            for l in range(1, levels):
                panel_send(l, c, j, 0, per_dev).wait_send()
        for l in range(levels):
            out_copy(l, c).wait()


def body(right_side, prior, lower_blocks, inverse_diag, fill_cols):
    levels, per_dev, rhs, order = right_side.shape
    fills = fill_cols.shape[2]
    width = rhs // CHUNKS
    f32 = jnp.float32
    dma = pltpu.SemaphoreType.DMA
    any_space = pl.BlockSpec(memory_space=pl.ANY)
    return pl.pallas_call(
        kernel,
        out_shape=jax.ShapeDtypeStruct(right_side.shape, f32),
        in_specs=[any_space] * 4 + [pl.BlockSpec(memory_space=pltpu.SMEM)],
        out_specs=any_space,
        scratch_shapes=[
            [
                [pltpu.VMEM((3 * per_dev, width, order), f32) for _ in range(CHUNKS)]
                for _ in range(levels)
            ],
            [pltpu.VMEM((per_dev, width, order), f32) for _ in range(CHUNKS)],
            pltpu.VMEM(right_side.shape, f32),
            pltpu.VMEM((STAGE, fills + 1, order, order), f32),
            pltpu.VMEM((KEPT, per_dev, fills + 1, order, order), jnp.bfloat16),
            pltpu.VMEM((KEPT, per_dev, fills + 1, order, order), jnp.bfloat16),
            dma((2, STAGE)),
            dma((levels,)),
            dma((CHUNKS,)),
            dma((levels, CHUNKS, 2)),
            dma((levels, CHUNKS, 2)),
            dma((levels, CHUNKS)),
        ],
        compiler_params=pltpu.CompilerParams(
            collective_id=0, has_side_effects=True, vmem_limit_bytes=60 << 20
        ),
    )(right_side, prior, lower_blocks, inverse_diag, fill_cols)


def solution(mesh):
    return jax.shard_map(
        body,
        mesh=mesh,
        in_specs=(
            P(None, "rows", "rhs", None),
            P("rows", "rhs", None),
            P(None, "rows", None, None, None),
            P(None, "rows", None, None),
            P(None, "rows", None),
        ),
        out_specs=P(None, "rows", "rhs", None),
        check_vma=False,
    )
```

```python
import functools

import jax
import jax.numpy as jnp
from jax import lax
from jax.experimental import pallas as pl
from jax.experimental.pallas import tpu as pltpu
from jax.sharding import PartitionSpec as P

CHUNKS = 2
STAGE = 16
KEPT = 2


def split(x):
    high = x.astype(jnp.bfloat16)
    low = (x - high.astype(jnp.float32)).astype(jnp.bfloat16)
    return high, low


def product(panel, high, low):
    count = panel.shape[0]
    panel_high, panel_low = split(panel)
    both = jnp.dot(
        jnp.concatenate([panel_high, panel_low], axis=0), high, preferred_element_type=jnp.float32
    )
    cross = jnp.dot(panel_high, low, preferred_element_type=jnp.float32)
    return both[:count] + both[count:] + cross


def kernel(
    right_hbm, prior_hbm, lower_hbm, inverse_hbm, fill_hbm, out_hbm,
    fill, tables, last, right, stage, high_blocks, low_blocks,
    fill_sem, stage_sem, right_sem, prior_sem, send_sem, recv_sem, out_sem,
):
    levels, per_dev, fills = fill.shape
    devices = lax.axis_size("rows")
    bits = devices.bit_length() - 1
    me = lax.axis_index("rows")
    width = right.shape[2] // CHUNKS
    units = levels * per_dev
    partners = [
        [jnp.bitwise_xor(me, 1 << (2 * l + j) % bits) for j in range(2)] for l in range(levels)
    ]

    def stage_copies(unit):
        level, row, slot = unit // per_dev, unit % per_dev, unit % STAGE
        return (
            pltpu.make_async_copy(
                lower_hbm.at[level, row], stage.at[slot, pl.ds(0, fills)], stage_sem.at[0, slot]
            ),
            pltpu.make_async_copy(
                inverse_hbm.at[level, row], stage.at[slot, fills], stage_sem.at[1, slot]
            ),
        )

    def rows_of(c):
        return pl.ds(c * width, width)

    def prior_send(c, j):
        return pltpu.make_async_remote_copy(
            src_ref=prior_hbm.at[:, rows_of(c)],
            dst_ref=tables[0][c].at[pl.ds((j + 1) * per_dev, per_dev)],
            send_sem=send_sem.at[0, c, j],
            recv_sem=recv_sem.at[0, c, j],
            device_id={"rows": partners[0][j]},
            device_id_type=pl.DeviceIdType.MESH,
        )

    def panel_send(l, c, j, first, count):
        table = tables[l][c]
        return pltpu.make_async_remote_copy(
            src_ref=table.at[pl.ds(first, count)],
            dst_ref=table.at[pl.ds((j + 1) * per_dev + first, count)],
            send_sem=send_sem.at[l, c, j],
            recv_sem=recv_sem.at[l, c, j],
            device_id={"rows": partners[l][j]},
            device_id_type=pl.DeviceIdType.MESH,
        )

    def solved(l, c):
        return last[c] if l == levels - 1 else tables[l + 1][c].at[pl.ds(0, per_dev)]

    def out_copy(l, c):
        return pltpu.make_async_copy(
            solved(l, c), out_hbm.at[l, :, rows_of(c)], out_sem.at[l, c]
        )

    def prior_copy(c):
        return pltpu.make_async_copy(
            prior_hbm.at[:, rows_of(c)], tables[0][c].at[pl.ds(0, per_dev)], prior_sem.at[c]
        )

    def right_copy(l):
        return pltpu.make_async_copy(right_hbm.at[l], right.at[l], right_sem.at[l])

    def convert(level):
        kept = level % KEPT

        def one(row, carry):
            unit = level * per_dev + row
            slot = unit % STAGE
            for copy in stage_copies(unit):
                copy.wait()

            def block(b, inner):
                high, low = split(stage[slot, b].T)
                high_blocks[kept, row, b] = high
                low_blocks[kept, row, b] = low
                return inner

            lax.fori_loop(0, fills + 1, block, 0)

            @pl.when(unit + STAGE < units)
            def _():
                for copy in stage_copies(unit + STAGE):
                    copy.start()

            return carry

        lax.fori_loop(0, per_dev, one, 0)

    def step(l, c):
        kept = l % KEPT
        if l == 0:
            prior_copy(c).wait()
        if c == 0:
            right_copy(l).wait()
        for j in range(2):
            panel_send(l, c, j, 0, per_dev).wait_recv()
        table = tables[l][c]

        def one(row, carry):
            panels = []
            for f in range(fills):
                column = fill[l, row, f]
                relative = jnp.maximum(column - l * devices * per_dev, 0)
                holder, within = relative // per_dev, relative % per_dev
                group = jnp.where(
                    holder == me, 0, jnp.where(holder == partners[l][0], 1, 2)
                )
                filled = jnp.where(column >= 0, 1.0, 0.0).astype(jnp.float32)
                panels.append(table[group * per_dev + within] * filled)
            order = right.shape[3]
            total = product(
                jnp.concatenate(panels, axis=1),
                high_blocks[kept, row, :fills].reshape(fills * order, order),
                low_blocks[kept, row, :fills].reshape(fills * order, order),
            )
            reduced = right[l, row, rows_of(c)] - total
            current = product(
                reduced, high_blocks[kept, row, fills], low_blocks[kept, row, fills]
            )
            if l == levels - 1:
                last[c][row] = current
            else:
                tables[l + 1][c][row] = current
                for j in range(2):
                    panel_send(l + 1, c, j, row, 1).start()
            return carry

        lax.fori_loop(0, per_dev, one, 0)
        out_copy(l, c).start()

    fill_copy = pltpu.make_async_copy(fill_hbm, fill, fill_sem)
    fill_copy.start()
    for unit in range(min(STAGE, units)):
        for copy in stage_copies(unit):
            copy.start()
    for c in range(CHUNKS):
        prior_copy(c).start()
    for l in range(levels):
        right_copy(l).start()

    barrier = pltpu.get_barrier_semaphore()
    for bit in range(bits):
        pl.semaphore_signal(
            barrier,
            inc=1,
            device_id={"rows": jnp.bitwise_xor(me, 1 << bit)},
            device_id_type=pl.DeviceIdType.MESH,
        )
    pl.semaphore_wait(barrier, bits)

    for c in range(CHUNKS):
        for j in range(2):
            prior_send(c, j).start()
    fill_copy.wait()
    convert(0)
    for l in range(levels):
        for c in range(CHUNKS):
            step(l, c)
            if l == 0 and c == 0 and levels > 1:
                convert(1)
        if l + KEPT < levels:
            convert(l + KEPT)
    for c in range(CHUNKS):
        for j in range(2):
            prior_send(c, j).wait_send()
            for l in range(1, levels):
                panel_send(l, c, j, 0, per_dev).wait_send()
        for l in range(levels):
            out_copy(l, c).wait()


def body(right_side, prior, lower_blocks, inverse_diag, fill_cols):
    levels, per_dev, rhs, order = right_side.shape
    fills = fill_cols.shape[2]
    width = rhs // CHUNKS
    f32 = jnp.float32
    dma = pltpu.SemaphoreType.DMA
    any_space = pl.BlockSpec(memory_space=pl.ANY)
    return pl.pallas_call(
        kernel,
        out_shape=jax.ShapeDtypeStruct(right_side.shape, f32),
        in_specs=[any_space] * 5,
        out_specs=any_space,
        scratch_shapes=[
            pltpu.SMEM(fill_cols.shape, jnp.int32),
            [
                [pltpu.VMEM((3 * per_dev, width, order), f32) for _ in range(CHUNKS)]
                for _ in range(levels)
            ],
            [pltpu.VMEM((per_dev, width, order), f32) for _ in range(CHUNKS)],
            pltpu.VMEM(right_side.shape, f32),
            pltpu.VMEM((STAGE, fills + 1, order, order), f32),
            pltpu.VMEM((KEPT, per_dev, fills + 1, order, order), jnp.bfloat16),
            pltpu.VMEM((KEPT, per_dev, fills + 1, order, order), jnp.bfloat16),
            dma,
            dma((2, STAGE)),
            dma((levels,)),
            dma((CHUNKS,)),
            dma((levels, CHUNKS, 2)),
            dma((levels, CHUNKS, 2)),
            dma((levels, CHUNKS)),
        ],
        compiler_params=pltpu.CompilerParams(
            collective_id=0, has_side_effects=True, vmem_limit_bytes=60 << 20
        ),
    )(right_side, prior, lower_blocks, inverse_diag, fill_cols)


def solution(mesh):
    return jax.shard_map(
        body,
        mesh=mesh,
        in_specs=(
            P(None, "rows", "rhs", None),
            P("rows", "rhs", None),
            P(None, "rows", None, None, None),
            P(None, "rows", None, None),
            P(None, "rows", None),
        ),
        out_specs=P(None, "rows", "rhs", None),
        check_vma=False,
    )
```

```python
import functools

import jax
import jax.numpy as jnp
from jax import lax
from jax.experimental import pallas as pl
from jax.experimental.pallas import tpu as pltpu
from jax.sharding import PartitionSpec as P

CHUNKS = 2
STAGE = 16
KEPT = 2


def split(x):
    high = x.astype(jnp.bfloat16)
    low = (x - high.astype(jnp.float32)).astype(jnp.bfloat16)
    return high, low


def product(panel, high, low):
    count = panel.shape[0]
    panel_high, panel_low = split(panel)
    both = jnp.dot(
        jnp.concatenate([panel_high, panel_low], axis=0), high, preferred_element_type=jnp.float32
    )
    cross = jnp.dot(panel_high, low, preferred_element_type=jnp.float32)
    return both[:count] + both[count:] + cross


def kernel(
    right_hbm, prior_hbm, lower_hbm, inverse_hbm, fill_hbm, out_hbm,
    fill, tables, last, right, stage, high_blocks, low_blocks,
    fill_sem, stage_sem, right_sem, prior_sem, send_sem, recv_sem, out_sem,
):
    levels, per_dev, fills = fill.shape
    devices = lax.axis_size("rows")
    bits = devices.bit_length() - 1
    me = lax.axis_index("rows")
    width = right.shape[2] // CHUNKS
    units = levels * per_dev
    partners = [
        [jnp.bitwise_xor(me, 1 << (2 * l + j) % bits) for j in range(2)] for l in range(levels)
    ]

    def stage_copies(unit):
        level, row, slot = unit // per_dev, unit % per_dev, unit % STAGE
        return (
            pltpu.make_async_copy(
                lower_hbm.at[level, row], stage.at[slot, pl.ds(0, fills)], stage_sem.at[0, slot]
            ),
            pltpu.make_async_copy(
                inverse_hbm.at[level, row], stage.at[slot, fills], stage_sem.at[1, slot]
            ),
        )

    def rows_of(c):
        return pl.ds(c * width, width)

    def prior_send(c, j):
        return pltpu.make_async_remote_copy(
            src_ref=prior_hbm.at[:, rows_of(c)],
            dst_ref=tables[0][c].at[pl.ds((j + 1) * per_dev, per_dev)],
            send_sem=send_sem.at[0, c, j],
            recv_sem=recv_sem.at[0, c, j],
            device_id={"rows": partners[0][j]},
            device_id_type=pl.DeviceIdType.MESH,
        )

    def panel_send(l, c, j, first, count):
        table = tables[l][c]
        return pltpu.make_async_remote_copy(
            src_ref=table.at[pl.ds(first, count)],
            dst_ref=table.at[pl.ds((j + 1) * per_dev + first, count)],
            send_sem=send_sem.at[l, c, j],
            recv_sem=recv_sem.at[l, c, j],
            device_id={"rows": partners[l][j]},
            device_id_type=pl.DeviceIdType.MESH,
        )

    def solved(l, c):
        return last[c] if l == levels - 1 else tables[l + 1][c].at[pl.ds(0, per_dev)]

    def out_copy(l, c):
        return pltpu.make_async_copy(
            solved(l, c), out_hbm.at[l, :, rows_of(c)], out_sem.at[l, c]
        )

    def prior_copy(c):
        return pltpu.make_async_copy(
            prior_hbm.at[:, rows_of(c)], tables[0][c].at[pl.ds(0, per_dev)], prior_sem.at[c]
        )

    def right_copy(l):
        return pltpu.make_async_copy(right_hbm.at[l], right.at[l], right_sem.at[l])

    def convert(level):
        kept = level % KEPT

        def one(row, carry):
            unit = level * per_dev + row
            slot = unit % STAGE
            for copy in stage_copies(unit):
                copy.wait()

            def block(b, inner):
                high, low = split(stage[slot, b].T)
                high_blocks[kept, row, b] = high
                low_blocks[kept, row, b] = low
                return inner

            lax.fori_loop(0, fills + 1, block, 0, unroll=5)

            @pl.when(unit + STAGE < units)
            def _():
                for copy in stage_copies(unit + STAGE):
                    copy.start()

            return carry

        lax.fori_loop(0, per_dev, one, 0)

    def step(l, c):
        kept = l % KEPT
        if l == 0:
            prior_copy(c).wait()
        if c == 0:
            right_copy(l).wait()
        for j in range(2):
            panel_send(l, c, j, 0, per_dev).wait_recv()
        table = tables[l][c]

        def one(row, carry):
            panels = []
            for f in range(fills):
                column = fill[l, row, f]
                relative = jnp.maximum(column - l * devices * per_dev, 0)
                holder, within = relative // per_dev, relative % per_dev
                group = jnp.where(
                    holder == me, 0, jnp.where(holder == partners[l][0], 1, 2)
                )
                filled = jnp.where(column >= 0, 1.0, 0.0).astype(jnp.float32)
                panels.append(table[group * per_dev + within] * filled)
            order = right.shape[3]
            total = product(
                jnp.concatenate(panels, axis=1),
                high_blocks[kept, row, :fills].reshape(fills * order, order),
                low_blocks[kept, row, :fills].reshape(fills * order, order),
            )
            reduced = right[l, row, rows_of(c)] - total
            current = product(
                reduced, high_blocks[kept, row, fills], low_blocks[kept, row, fills]
            )
            if l == levels - 1:
                last[c][row] = current
            else:
                tables[l + 1][c][row] = current
                for j in range(2):
                    panel_send(l + 1, c, j, row, 1).start()
            return carry

        lax.fori_loop(0, per_dev, one, 0)
        out_copy(l, c).start()

    fill_copy = pltpu.make_async_copy(fill_hbm, fill, fill_sem)
    fill_copy.start()
    for unit in range(min(STAGE, units)):
        for copy in stage_copies(unit):
            copy.start()
    for c in range(CHUNKS):
        prior_copy(c).start()
    for l in range(levels):
        right_copy(l).start()

    barrier = pltpu.get_barrier_semaphore()
    for bit in range(bits):
        pl.semaphore_signal(
            barrier,
            inc=1,
            device_id={"rows": jnp.bitwise_xor(me, 1 << bit)},
            device_id_type=pl.DeviceIdType.MESH,
        )
    pl.semaphore_wait(barrier, bits)

    for c in range(CHUNKS):
        for j in range(2):
            prior_send(c, j).start()
    fill_copy.wait()
    convert(0)
    for l in range(levels):
        for c in range(CHUNKS):
            step(l, c)
            if l > 0 and c == 0 and l + 1 < levels:
                convert(l + 1)
        if l == 0 and levels > 1:
            convert(1)
    for c in range(CHUNKS):
        for j in range(2):
            prior_send(c, j).wait_send()
            for l in range(1, levels):
                panel_send(l, c, j, 0, per_dev).wait_send()
        for l in range(levels):
            out_copy(l, c).wait()


def body(right_side, prior, lower_blocks, inverse_diag, fill_cols):
    levels, per_dev, rhs, order = right_side.shape
    fills = fill_cols.shape[2]
    width = rhs // CHUNKS
    f32 = jnp.float32
    dma = pltpu.SemaphoreType.DMA
    any_space = pl.BlockSpec(memory_space=pl.ANY)
    return pl.pallas_call(
        kernel,
        out_shape=jax.ShapeDtypeStruct(right_side.shape, f32),
        in_specs=[any_space] * 5,
        out_specs=any_space,
        scratch_shapes=[
            pltpu.SMEM(fill_cols.shape, jnp.int32),
            [
                [pltpu.VMEM((3 * per_dev, width, order), f32) for _ in range(CHUNKS)]
                for _ in range(levels)
            ],
            [pltpu.VMEM((per_dev, width, order), f32) for _ in range(CHUNKS)],
            pltpu.VMEM(right_side.shape, f32),
            pltpu.VMEM((STAGE, fills + 1, order, order), f32),
            pltpu.VMEM((KEPT, per_dev, fills + 1, order, order), jnp.bfloat16),
            pltpu.VMEM((KEPT, per_dev, fills + 1, order, order), jnp.bfloat16),
            dma,
            dma((2, STAGE)),
            dma((levels,)),
            dma((CHUNKS,)),
            dma((levels, CHUNKS, 2)),
            dma((levels, CHUNKS, 2)),
            dma((levels, CHUNKS)),
        ],
        compiler_params=pltpu.CompilerParams(
            collective_id=0, has_side_effects=True, vmem_limit_bytes=60 << 20
        ),
    )(right_side, prior, lower_blocks, inverse_diag, fill_cols)


def solution(mesh):
    return jax.shard_map(
        body,
        mesh=mesh,
        in_specs=(
            P(None, "rows", "rhs", None),
            P("rows", "rhs", None),
            P(None, "rows", None, None, None),
            P(None, "rows", None, None),
            P(None, "rows", None),
        ),
        out_specs=P(None, "rows", "rhs", None),
        check_vma=False,
    )
```

```python
import functools

import jax
import jax.numpy as jnp
from jax import lax
from jax.experimental import pallas as pl
from jax.experimental.pallas import tpu as pltpu
from jax.sharding import PartitionSpec as P

CHUNKS = 2
STAGE = 16
KEPT = 2


def split(x):
    high = x.astype(jnp.bfloat16)
    low = (x - high.astype(jnp.float32)).astype(jnp.bfloat16)
    return high, low


def product(panel, high, low):
    count = panel.shape[0]
    panel_high, panel_low = split(panel)
    both = jnp.dot(
        jnp.concatenate([panel_high, panel_low], axis=0), high, preferred_element_type=jnp.float32
    )
    cross = jnp.dot(panel_high, low, preferred_element_type=jnp.float32)
    return both[:count] + both[count:] + cross


def kernel(
    right_hbm, prior_hbm, lower_hbm, inverse_hbm, fill_hbm, out_hbm,
    fill, tables, last, right, stage, high_blocks, low_blocks,
    fill_sem, stage_sem, right_sem, prior_sem, send_sem, recv_sem, out_sem,
):
    levels, per_dev, fills = fill.shape
    devices = lax.axis_size("rows")
    bits = devices.bit_length() - 1
    me = lax.axis_index("rows")
    width = right.shape[2] // CHUNKS
    units = levels * per_dev
    partners = [
        [jnp.bitwise_xor(me, 1 << (2 * l + j) % bits) for j in range(2)] for l in range(levels)
    ]

    def stage_copies(unit):
        level, row, slot = unit // per_dev, unit % per_dev, unit % STAGE
        return (
            pltpu.make_async_copy(
                lower_hbm.at[level, row], stage.at[slot, pl.ds(0, fills)], stage_sem.at[0, slot]
            ),
            pltpu.make_async_copy(
                inverse_hbm.at[level, row], stage.at[slot, fills], stage_sem.at[1, slot]
            ),
        )

    def rows_of(c):
        return pl.ds(c * width, width)

    def prior_send(c, j):
        return pltpu.make_async_remote_copy(
            src_ref=prior_hbm.at[:, rows_of(c)],
            dst_ref=tables[0][c].at[pl.ds((j + 1) * per_dev, per_dev)],
            send_sem=send_sem.at[0, c, j],
            recv_sem=recv_sem.at[0, c, j],
            device_id={"rows": partners[0][j]},
            device_id_type=pl.DeviceIdType.MESH,
        )

    def panel_send(l, c, j, first, count):
        table = tables[l][c]
        return pltpu.make_async_remote_copy(
            src_ref=table.at[pl.ds(first, count)],
            dst_ref=table.at[pl.ds((j + 1) * per_dev + first, count)],
            send_sem=send_sem.at[l, c, j],
            recv_sem=recv_sem.at[l, c, j],
            device_id={"rows": partners[l][j]},
            device_id_type=pl.DeviceIdType.MESH,
        )

    def solved(l, c):
        return last[c] if l == levels - 1 else tables[l + 1][c].at[pl.ds(0, per_dev)]

    def out_copy(l, c):
        return pltpu.make_async_copy(
            solved(l, c), out_hbm.at[l, :, rows_of(c)], out_sem.at[l, c]
        )

    def prior_copy(c):
        return pltpu.make_async_copy(
            prior_hbm.at[:, rows_of(c)], tables[0][c].at[pl.ds(0, per_dev)], prior_sem.at[c]
        )

    def right_copy(l):
        return pltpu.make_async_copy(right_hbm.at[l], right.at[l], right_sem.at[l])

    def convert(level):
        kept = level % KEPT

        def one(row, carry):
            unit = level * per_dev + row
            slot = unit % STAGE
            for copy in stage_copies(unit):
                copy.wait()

            def block(b, inner):
                high, low = split(stage[slot, b].T)
                high_blocks[kept, row, b] = high
                low_blocks[kept, row, b] = low
                return inner

            lax.fori_loop(0, fills + 1, block, 0, unroll=5)

            @pl.when(unit + STAGE < units)
            def _():
                for copy in stage_copies(unit + STAGE):
                    copy.start()

            return carry

        lax.fori_loop(0, per_dev, one, 0)

    def step(l, c):
        kept = l % KEPT
        if l == 0:
            prior_copy(c).wait()
        if c == 0:
            right_copy(l).wait()
        for j in range(2):
            panel_send(l, c, j, 0, per_dev).wait_recv()
        table = tables[l][c]

        def one(row, carry):
            panels = []
            for f in range(fills):
                column = fill[l, row, f]
                relative = jnp.maximum(column - l * devices * per_dev, 0)
                holder, within = relative // per_dev, relative % per_dev
                group = jnp.where(
                    holder == me, 0, jnp.where(holder == partners[l][0], 1, 2)
                )
                filled = jnp.where(column >= 0, 1.0, 0.0).astype(jnp.float32)
                panels.append(table[group * per_dev + within] * filled)
            order = right.shape[3]
            total = product(
                jnp.concatenate(panels, axis=1),
                high_blocks[kept, row, :fills].reshape(fills * order, order),
                low_blocks[kept, row, :fills].reshape(fills * order, order),
            )
            reduced = right[l, row, rows_of(c)] - total
            current = product(
                reduced, high_blocks[kept, row, fills], low_blocks[kept, row, fills]
            )
            if l == levels - 1:
                last[c][row] = current
                pltpu.make_async_copy(
                    last[c].at[row], out_hbm.at[l, row, rows_of(c)], out_sem.at[l, c]
                ).start()
            else:
                tables[l + 1][c][row] = current
                for j in range(2):
                    panel_send(l + 1, c, j, row, 1).start()
            return carry

        lax.fori_loop(0, per_dev, one, 0)
        if l < levels - 1:
            out_copy(l, c).start()

    barrier = pltpu.get_barrier_semaphore()
    for bit in range(bits):
        pl.semaphore_signal(
            barrier,
            inc=1,
            device_id={"rows": jnp.bitwise_xor(me, 1 << bit)},
            device_id_type=pl.DeviceIdType.MESH,
        )
    fill_copy = pltpu.make_async_copy(fill_hbm, fill, fill_sem)
    fill_copy.start()
    for c in range(CHUNKS):
        prior_copy(c).start()
    for l in range(levels):
        right_copy(l).start()
    for unit in range(min(per_dev, units)):
        for copy in stage_copies(unit):
            copy.start()
    pl.semaphore_wait(barrier, bits)

    for c in range(CHUNKS):
        for j in range(2):
            prior_send(c, j).start()
    for unit in range(min(per_dev, units), min(STAGE, units)):
        for copy in stage_copies(unit):
            copy.start()
    fill_copy.wait()
    convert(0)
    for l in range(levels):
        for c in range(CHUNKS):
            step(l, c)
            if l > 0 and c == 0 and l + 1 < levels:
                convert(l + 1)
        if l == 0 and levels > 1:
            convert(1)
    for c in range(CHUNKS):
        for j in range(2):
            prior_send(c, j).wait_send()
            for l in range(1, levels):
                panel_send(l, c, j, 0, per_dev).wait_send()
        for l in range(levels):
            out_copy(l, c).wait()


def body(right_side, prior, lower_blocks, inverse_diag, fill_cols):
    levels, per_dev, rhs, order = right_side.shape
    fills = fill_cols.shape[2]
    width = rhs // CHUNKS
    f32 = jnp.float32
    dma = pltpu.SemaphoreType.DMA
    any_space = pl.BlockSpec(memory_space=pl.ANY)
    return pl.pallas_call(
        kernel,
        out_shape=jax.ShapeDtypeStruct(right_side.shape, f32),
        in_specs=[any_space] * 5,
        out_specs=any_space,
        scratch_shapes=[
            pltpu.SMEM(fill_cols.shape, jnp.int32),
            [
                [pltpu.VMEM((3 * per_dev, width, order), f32) for _ in range(CHUNKS)]
                for _ in range(levels)
            ],
            [pltpu.VMEM((per_dev, width, order), f32) for _ in range(CHUNKS)],
            pltpu.VMEM(right_side.shape, f32),
            pltpu.VMEM((STAGE, fills + 1, order, order), f32),
            pltpu.VMEM((KEPT, per_dev, fills + 1, order, order), jnp.bfloat16),
            pltpu.VMEM((KEPT, per_dev, fills + 1, order, order), jnp.bfloat16),
            dma,
            dma((2, STAGE)),
            dma((levels,)),
            dma((CHUNKS,)),
            dma((levels, CHUNKS, 2)),
            dma((levels, CHUNKS, 2)),
            dma((levels, CHUNKS)),
        ],
        compiler_params=pltpu.CompilerParams(
            collective_id=0, has_side_effects=True, vmem_limit_bytes=60 << 20
        ),
    )(right_side, prior, lower_blocks, inverse_diag, fill_cols)


def solution(mesh):
    return jax.shard_map(
        body,
        mesh=mesh,
        in_specs=(
            P(None, "rows", "rhs", None),
            P("rows", "rhs", None),
            P(None, "rows", None, None, None),
            P(None, "rows", None, None),
            P(None, "rows", None),
        ),
        out_specs=P(None, "rows", "rhs", None),
        check_vma=False,
    )
```
